32 devices in a mesh: inst: 4 (over x, core), lab: 8 (over z, y).
Axes of the slice: x: 2, y: 2, z: 4, core: 2. Of those that a mesh axis runs over, the one named last changes fastest.
Arguments:
- features: bfloat16 [2048, 768], P('inst'), may hold values from -6 to 6
- tile_rows: int32 [128], P(('inst', 'lab')), may hold values from 0 to 1, as said below
- tile_labels: int32 [128], P(('inst', 'lab')), may hold values from 0 to 3
- tile_values: bfloat16 [128, 256, 256], P(('inst', 'lab')), may hold values from 0 to 1
- cluster_ids: int32 [8192], P(('lab', 'inst')), may hold values from 0 to 1023, as said below
Outputs:
- label_embed: float32 [8192, 768], P(('lab', 'inst'))
- centroids: float32 [1024, 768], P(('inst', 'lab'))
The draws below stay inside these ranges and needn't reach their ends.
Inputs may be any that keep to these rules, and one draw needn't show every extreme that they name: Within each block of 4 entries the pairs (tile_rows, tile_labels) are distinct. Within each aligned block of 256 labels, at most 16 labels have clusters with the same value of cluster_ids // 32, and that many is reached in every block.
All inputs are finite; a program needn't handle non-finite values.
Results may differ from the reference program's by a relative error of at most 0.01.
Values may be sent and summed in bfloat16 or wider, within the bound.
A program may use at most 128 MiB of HBM per device.

```python
import jax
import jax.numpy as jnp
from jax import lax

D = 768
TILE = 256
INST_DEV = 512
LAB_DEV = 256
CL_OWN = 32
OWNERS = 32
RT = 2
LT = 4
NT_DEV = 4
TILES = 128
INSTANCES = 2048
CLUST = 1024
N_INST = 4
N_LAB = 8


def tile_pairs(key):
    keys = jax.random.split(jax.random.fold_in(key, 17), OWNERS)

    def pick(single):
        return jax.random.permutation(single, RT * LT)[:NT_DEV]
    picks = jax.vmap(pick)(keys).reshape(-1).astype(jnp.int32)
    return (picks // LT, picks % LT)


def draw_tile_rows(key, part):
    return tile_pairs(key)[0]


def draw_tile_labels(key, part):
    return tile_pairs(key)[1]


def draw_cluster_ids(key, part):
    keys = jax.random.split(jax.random.fold_in(key, 5), OWNERS)
    lowest = max(1, OWNERS // 16)

    def block(single):
        first, second, third, fourth = jax.random.split(single, 4)
        order = jax.random.permutation(first, OWNERS).astype(jnp.int32)
        doubled = jax.random.randint(second, (), lowest, OWNERS // 2 + 1)
        ranks = jnp.arange(LAB_DEV, dtype=jnp.int32) % OWNERS
        ranks = jnp.where(ranks >= OWNERS - doubled, ranks - (OWNERS - doubled), ranks)
        owner = order[ranks]
        inside = jax.random.randint(third, (LAB_DEV,), 0, CL_OWN)
        return jax.random.permutation(fourth, owner * CL_OWN + inside)
    return jax.vmap(block)(keys).reshape(-1).astype(jnp.int32)


def block_scale(own_key, dims, cuts, least, largest):
    def one(axis_at, blocks):
        steps = jax.random.uniform(jax.random.fold_in(jax.random.fold_in(own_key, 6), axis_at), (blocks,), jnp.float32, least / len(cuts), largest / len(cuts))
        return jnp.repeat(jnp.exp(steps), dims[axis_at] // blocks).reshape((-1,) + (1,) * (len(dims) - axis_at - 1))

    level = one(*cuts[0])
    for cut in cuts[1:]:
        level = level * one(*cut)
    return level


def normal_values(own_key, extent, width, reach, cuts=(), kind=jnp.bfloat16):
    level = block_scale(own_key, extent, cuts, -0.22, 0.18) if cuts else 1.0
    values = jax.random.normal(own_key, extent, jnp.float32) * width * level
    return jnp.minimum(jnp.maximum(values, -reach), reach).astype(kind)


def setup_inputs(seed: int = 0) -> dict:
    seeds = jax.random.split(jax.random.key(seed), 6)
    features = normal_values(seeds[0], (INSTANCES, D), 1.0, 6.0, ((0, 4),))
    tile_rows = draw_tile_rows(jax.random.fold_in(seeds[5], 71), 0)
    tile_labels = draw_tile_labels(jax.random.fold_in(seeds[5], 71), 0)
    tile_values = jnp.clip(1.0 * jax.random.uniform(seeds[3], (TILES, TILE, TILE), jnp.float32) ** block_scale(seeds[3], (TILES, TILE, TILE), ((0, 32),), -0.2, 0.2), 0.0, 1.0).astype(jnp.bfloat16)
    cluster_ids = draw_cluster_ids(jax.random.fold_in(seeds[5], 71), 0)
    return {"features": features, "tile_rows": tile_rows, "tile_labels": tile_labels, "tile_values": tile_values, "cluster_ids": cluster_ids}


def unit_rows(matrix):
    return matrix * lax.rsqrt(lax.optimization_barrier(jnp.sum(matrix * matrix, axis=-1, keepdims=True)) + 1e-06)

def reference(features, tile_rows, tile_labels, tile_values, cluster_ids):
    normed = unit_rows(features.astype(jnp.float32)).astype(jnp.bfloat16)
    row_tiles = INST_DEV // TILE
    lab_tiles = LAB_DEV * N_INST // TILE
    block_rows = LAB_DEV * N_INST
    shard_x = normed.reshape(N_INST, row_tiles, TILE, D)
    rows_all = tile_rows.reshape(N_INST, N_LAB, NT_DEV)
    labs_all = tile_labels.reshape(N_INST, N_LAB, NT_DEV)
    vals_all = tile_values.reshape(N_INST, N_LAB, NT_DEV, TILE, TILE)

    def shard_step(carry, pieces):
        xs, rr, cc, vv = pieces

        def one_block(parts):
            row_ids, lab_ids, values = parts
            picked = xs[row_ids].astype(jnp.float32)
            prod = jnp.einsum('nrl,nrd->nld', values.astype(jnp.float32), picked)
            seg = jax.ops.segment_sum(prod, lab_ids, num_segments=lab_tiles)
            return seg.reshape(block_rows, D).astype(jnp.bfloat16)
        partial_value = lax.map(one_block, (rr, cc, vv))
        return (carry + partial_value.astype(jnp.float32), None)
    start = jnp.zeros((N_LAB, block_rows, D), jnp.float32)
    summed, _ = lax.scan(shard_step, start, (shard_x, rows_all, labs_all, vals_all))
    label_embed = unit_rows(summed.reshape(N_LAB * block_rows, D))
    cluster_sums = jax.ops.segment_sum(label_embed, cluster_ids, num_segments=CLUST)
    return (label_embed, unit_rows(cluster_sums))
```

```python
import functools

import jax
import jax.numpy as jnp
from jax import lax
from jax.experimental import pallas as pl
from jax.experimental.pallas import tpu as pltpu
from jax.sharding import PartitionSpec as P

CL_OWN = 32
CHUNKS = 4
MESH = pl.DeviceIdType.MESH


def unit_rows(matrix):
    return matrix * lax.rsqrt(jnp.sum(matrix * matrix, axis=-1, keepdims=True) + 1e-06)


def kernel(
    nx, ny, nz,
    rows_ref, labs_ref, ids_ref, feat_ref, val_ref,
    emb_ref, cen_ref,
    xn, vt, csend, crecv, xsend, xrecv, total, e32, ebf,
    ca_s, ca_r, xa_s, xa_r, acc_a, ya_s, ya_r,
    cb_s, cb_r, yb_s, yb_r, acc_b, xb_s, xb_r,
    fin_a, fin_b, za_s, za_r, zb_s, zb_r,
    s_core, r_core, s_x, r_x, s_ca, r_ca, s_cb, r_cb,
    s_xa, r_xa, s_yb, r_yb, s_ya, r_ya, s_xb, r_xb, s_za, r_za, s_zb, r_zb, s_out,
):
    inst = lax.axis_index("inst")
    lab = lax.axis_index("lab")
    x, c = inst // 2, inst % 2
    z, y = lab // ny, lab % ny
    other = 1 - c
    tile = val_ref.shape[1]
    width = feat_ref.shape[1]
    half = width // 2
    row_tiles = feat_ref.shape[0] // tile
    n_tiles = val_ref.shape[0]
    part = tile // CHUNKS

    core_peer = (x * 2 + other, lab)
    x_at = lambda d: (x + d) % nx
    y_at = lambda d: (y + d) % ny
    z_at = lambda d: (z + d) % nz
    x_peer = lambda d: (x_at(d) * 2 + c, lab)
    y_peer = lambda d: (inst, z * ny + y_at(d))
    z_peer = lambda d: (inst, z_at(d) * ny + y)
    peers = [core_peer]
    peers += [x_peer(d) for d in range(1, nx)]
    peers += [y_peer(d) for d in range(1, ny)]
    peers += [z_peer(d) for d in range(1, nz)]

    barrier = pltpu.get_barrier_semaphore()
    for peer in peers:
        pl.semaphore_signal(barrier, inc=1, device_id=peer, device_id_type=MESH)

    def remote(src, dst, send, recv, peer):
        return pltpu.make_async_remote_copy(
            src_ref=src, dst_ref=dst, send_sem=send, recv_sem=recv,
            device_id=peer, device_id_type=MESH,
        )

    sent = []

    xn[...] = unit_rows(feat_ref[...].astype(jnp.float32)).astype(jnp.bfloat16)
    for n in range(n_tiles):
        vt[n] = val_ref[n].T
    vt[n_tiles] = jnp.zeros((tile, tile), jnp.bfloat16)

    def partial(label_tile):
        pieces = []
        for r in range(row_tiles):
            at = jnp.int32(n_tiles)
            for n in range(n_tiles):
                hit = jnp.logical_and(rows_ref[n] == r, labs_ref[n] == label_tile)
                at = jnp.where(hit, n, at)
            pieces.append(vt[at])
        lhs = jnp.concatenate(pieces, axis=1)
        return jnp.dot(lhs, xn[...], preferred_element_type=jnp.float32)

    def core_send(d):
        xp = x_at(d)
        csend[xp] = partial(xp * 2 + other).astype(jnp.bfloat16)
        copies = []
        for q in range(CHUNKS):
            rows = pl.ds(q * part, part)
            copy = remote(
                csend.at[xp, rows], crecv.at[xp, rows],
                s_core.at[xp, q], r_core.at[xp, q], core_peer,
            )
            copies.append(copy)
        return copies

    x_copies = {}
    for d in range(1, nx):
        copies = core_send(d)
        if d == 1:
            pl.semaphore_wait(barrier, len(peers))
        for copy in copies:
            copy.start()
        sent += copies
        total[...] = partial(x_at(d) * 2 + c)
        for q in range(CHUNKS):
            rows = pl.ds(q * part, part)
            copies[q].wait_recv()
            mixed = total[rows] + crecv[x_at(d), rows].astype(jnp.float32)
            xsend[d - 1, rows] = mixed.astype(jnp.bfloat16)
            copy = remote(
                xsend.at[d - 1, rows], xrecv.at[d - 1, rows],
                s_x.at[d - 1, q], r_x.at[d - 1, q], x_peer(d),
            )
            copy.start()
            x_copies[d, q] = copy
            sent.append(copy)
    copies = core_send(0)
    if nx == 1:
        pl.semaphore_wait(barrier, len(peers))
    for copy in copies:
        copy.start()
    sent += copies
    total[...] = partial(x * 2 + c)
    for q in range(CHUNKS):
        rows = pl.ds(q * part, part)
        copies[q].wait_recv()
        total[rows] += crecv[x, rows].astype(jnp.float32)

    outs = []
    for q in range(CHUNKS):
        rows = pl.ds(q * part, part)
        value = total[rows]
        for d in range(1, nx):
            x_copies[d, q].wait_recv()
            value += xrecv[d - 1, rows].astype(jnp.float32)
        value = unit_rows(value)
        e32[rows] = value
        ebf[rows] = value.astype(jnp.bfloat16)
        out = pltpu.make_async_copy(e32.at[rows], emb_ref.at[rows], s_out.at[q])
        out.start()
        outs.append(out)

    ids = ids_ref[...].reshape(1, 1, tile)
    zb = nz * CL_OWN
    within = (
        lax.broadcasted_iota(jnp.int32, (nz, CL_OWN, tile), 0) * (ny * CL_OWN)
        + lax.broadcasted_iota(jnp.int32, (nz, CL_OWN, tile), 1)
    )

    def picks(xp, cp, yp):
        base = ((xp * 2 + cp) * (nz * ny) + yp) * CL_OWN
        hit = jnp.where(within + base == ids, 1.0, 0.0)
        return hit.reshape(zb, tile).astype(jnp.bfloat16)

    def sums_a(xp, cp):
        member = jnp.concatenate([picks(xp, cp, yp) for yp in range(ny)], axis=0)
        out = jnp.dot(member, ebf[:, :half], preferred_element_type=jnp.float32)
        return out.reshape(ny, zb, half)

    def sums_b(yp, cp):
        member = jnp.concatenate([picks(xp, cp, yp) for xp in range(nx)], axis=0)
        out = jnp.dot(member, ebf[:, half:], preferred_element_type=jnp.float32)
        return out.reshape(nx, zb, half)

    core_a, core_b = {}, {}
    for d in [*range(1, max(nx, ny)), 0]:
        if d < nx:
            xp = x_at(d)
            ca_s[xp] = sums_a(xp, other).astype(jnp.bfloat16)
            core_a[d] = remote(ca_s.at[xp], ca_r.at[xp], s_ca.at[xp], r_ca.at[xp], core_peer)
            core_a[d].start()
        if d < ny:
            yp = y_at(d)
            cb_s[yp] = sums_b(yp, other).astype(jnp.bfloat16)
            core_b[d] = remote(cb_s.at[yp], cb_r.at[yp], s_cb.at[yp], r_cb.at[yp], core_peer)
            core_b[d].start()
    sent += [*core_a.values(), *core_b.values()]

    xa, yb = {}, {}
    for d in [*range(1, max(nx, ny)), 0]:
        if d < nx:
            xp = x_at(d)
            mine = sums_a(xp, c)
            core_a[d].wait_recv()
            mine = mine + ca_r[xp].astype(jnp.float32)
            if d:
                xa_s[d - 1] = mine.astype(jnp.bfloat16)
                for k in [*range(1, ny), 0]:
                    yp = y_at(k)
                    xa[d, k] = remote(
                        xa_s.at[d - 1, yp], xa_r.at[d - 1, yp],
                        s_xa.at[d - 1, yp], r_xa.at[d - 1, yp], x_peer(d),
                    )
                    xa[d, k].start()
            else:
                acc_a[...] = mine
        if d < ny:
            yp = y_at(d)
            mine = sums_b(yp, c)
            core_b[d].wait_recv()
            mine = mine + cb_r[yp].astype(jnp.float32)
            if d:
                yb_s[d - 1] = mine.astype(jnp.bfloat16)
                for k in [*range(1, nx), 0]:
                    xp = x_at(k)
                    yb[d, k] = remote(
                        yb_s.at[d - 1, xp], yb_r.at[d - 1, xp],
                        s_yb.at[d - 1, xp], r_yb.at[d - 1, xp], y_peer(d),
                    )
                    yb[d, k].start()
            else:
                acc_b[...] = mine
    sent += [*xa.values(), *yb.values()]

    ya, xb = {}, {}
    for k in [*range(1, max(nx, ny)), 0]:
        if k < ny:
            yp = y_at(k)
            mine = acc_a[yp]
            for d in range(1, nx):
                xa[d, k].wait_recv()
                mine += xa_r[d - 1, yp].astype(jnp.float32)
            if k:
                ya_s[k - 1] = mine.astype(jnp.bfloat16)
                ya[k] = remote(
                    ya_s.at[k - 1], ya_r.at[k - 1], s_ya.at[k - 1], r_ya.at[k - 1], y_peer(k)
                )
                ya[k].start()
            else:
                fin_a[...] = mine.reshape(nz, CL_OWN, half)
        if k < nx:
            xp = x_at(k)
            mine = acc_b[xp]
            for d in range(1, ny):
                yb[d, k].wait_recv()
                mine += yb_r[d - 1, xp].astype(jnp.float32)
            if k:
                xb_s[k - 1] = mine.astype(jnp.bfloat16)
                xb[k] = remote(
                    xb_s.at[k - 1], xb_r.at[k - 1], s_xb.at[k - 1], r_xb.at[k - 1], x_peer(k)
                )
                xb[k].start()
            else:
                fin_b[...] = mine.reshape(nz, CL_OWN, half)
    sent += [*ya.values(), *xb.values()]

    zs = []
    for fin, got, arrived, z_s, z_r, s_z, r_z in (
        (fin_a, ya, ya_r, za_s, za_r, s_za, r_za),
        (fin_b, xb, xb_r, zb_s, zb_r, s_zb, r_zb),
    ):
        mine = fin[...]
        for k, copy in got.items():
            copy.wait_recv()
            mine += arrived[k - 1].astype(jnp.float32).reshape(nz, CL_OWN, half)
        fin[...] = mine
        for d in range(1, nz):
            z_s[d - 1] = fin[z_at(d)].astype(jnp.bfloat16)
            copy = remote(
                z_s.at[d - 1], z_r.at[d - 1], s_z.at[d - 1], r_z.at[d - 1], z_peer(d)
            )
            copy.start()
            zs.append(copy)
    sent += zs

    sum_a, sum_b = fin_a[z], fin_b[z]
    for copy in zs:
        copy.wait_recv()
    for d in range(1, nz):
        sum_a += za_r[d - 1].astype(jnp.float32)
        sum_b += zb_r[d - 1].astype(jnp.float32)
    cen_ref[...] = unit_rows(jnp.concatenate([sum_a, sum_b], axis=1))

    for copy in sent:
        copy.wait_send()
    for out in outs:
        out.wait()


def shards(features, tile_rows, tile_labels, tile_values, cluster_ids):
    tile = tile_values.shape[1]
    width = features.shape[1]
    labels = cluster_ids.shape[0]
    n_inst, n_lab = lax.axis_size("inst"), lax.axis_size("lab")
    nx = n_inst // 2
    ny = nx if n_lab % nx == 0 else 1
    nz = n_lab // ny
    assert labels == tile
    half = width // 2
    zb = nz * CL_OWN
    bf, f32 = jnp.bfloat16, jnp.float32
    ox, oy, oz = max(nx - 1, 1), max(ny - 1, 1), max(nz - 1, 1)
    dma = lambda *shape: [pltpu.SemaphoreType.DMA(shape)] * 2
    vmem = pl.BlockSpec(memory_space=pltpu.VMEM)
    smem = pl.BlockSpec(memory_space=pltpu.SMEM)
    return pl.pallas_call(
        functools.partial(kernel, nx, ny, nz),
        out_shape=(
            jax.ShapeDtypeStruct((labels, width), f32),
            jax.ShapeDtypeStruct((CL_OWN, width), f32),
        ),
        in_specs=[smem, smem, vmem, vmem, vmem],
        out_specs=(pl.BlockSpec(memory_space=pl.ANY), vmem),
        scratch_shapes=[
            pltpu.VMEM(features.shape, bf),
            pltpu.VMEM((tile_values.shape[0] + 1, tile, tile), bf),
            pltpu.VMEM((nx, tile, width), bf),
            pltpu.VMEM((nx, tile, width), bf),
            pltpu.VMEM((ox, tile, width), bf),
            pltpu.VMEM((ox, tile, width), bf),
            pltpu.VMEM((tile, width), f32),
            pltpu.VMEM((tile, width), f32),
            pltpu.VMEM((tile, width), bf),
            pltpu.VMEM((nx, ny, zb, half), bf),
            pltpu.VMEM((nx, ny, zb, half), bf),
            pltpu.VMEM((ox, ny, zb, half), bf),
            pltpu.VMEM((ox, ny, zb, half), bf),
            pltpu.VMEM((ny, zb, half), f32),
            pltpu.VMEM((oy, zb, half), bf),
            pltpu.VMEM((oy, zb, half), bf),
            pltpu.VMEM((ny, nx, zb, half), bf),
            pltpu.VMEM((ny, nx, zb, half), bf),
            pltpu.VMEM((oy, nx, zb, half), bf),
            pltpu.VMEM((oy, nx, zb, half), bf),
            pltpu.VMEM((nx, zb, half), f32),
            pltpu.VMEM((ox, zb, half), bf),
            pltpu.VMEM((ox, zb, half), bf),
            pltpu.VMEM((nz, CL_OWN, half), f32),
            pltpu.VMEM((nz, CL_OWN, half), f32),
            pltpu.VMEM((oz, CL_OWN, half), bf),
            pltpu.VMEM((oz, CL_OWN, half), bf),
            pltpu.VMEM((oz, CL_OWN, half), bf),
            pltpu.VMEM((oz, CL_OWN, half), bf),
            *dma(nx, CHUNKS),
            *dma(ox, CHUNKS),
            *dma(nx),
            *dma(ny),
            *dma(ox, ny),
            *dma(oy, nx),
            *dma(oy),
            *dma(ox),
            *dma(oz),
            *dma(oz),
            pltpu.SemaphoreType.DMA((CHUNKS,)),
        ],
        compiler_params=pltpu.CompilerParams(
            collective_id=0, has_side_effects=True, vmem_limit_bytes=60 * 1024 * 1024
        ),
        name="pifa_step",
    )(tile_rows, tile_labels, cluster_ids.reshape(1, labels), features, tile_values)


def solution(mesh):
    return jax.shard_map(
        shards,
        mesh=mesh,
        in_specs=(
            P("inst", None),
            P(("inst", "lab")),
            P(("inst", "lab")),
            P(("inst", "lab"), None, None),
            P(("lab", "inst")),
        ),
        out_specs=(P(("lab", "inst"), None), P(("inst", "lab"), None)),
        check_vma=False,
    )
```

```python
import functools

import jax
import jax.numpy as jnp
from jax import lax
from jax.experimental import pallas as pl
from jax.experimental.pallas import tpu as pltpu
from jax.sharding import PartitionSpec as P

CL_OWN = 32
CHUNKS = 8
PIECES = 3
MESH = pl.DeviceIdType.MESH


def unit_rows(matrix):
    return matrix * lax.rsqrt(jnp.sum(matrix * matrix, axis=-1, keepdims=True) + 1e-06)


def kernel(
    nx, ny, nz, pair,
    rows_ref, labs_ref, ids_ref, feat_ref, val_ref,
    emb_ref, cen_ref,
    xn, vt, csend, crecv, xsend, xrecv, total, ebf, ids_far, picks,
    ca_s, ca_r, xa_s, xa_r, acc_a, ya_s, ya_r,
    cb_s, cb_r, yb_s, yb_r, acc_b, xb_s, xb_r,
    fin_a, fin_b, za_s, za_r, zb_s, zb_r,
    s_core, r_core, s_x, r_x, s_ca, r_ca, s_cb, r_cb,
    s_xa, r_xa, s_yb, r_yb, s_ya, r_ya, s_xb, r_xb, s_za, r_za, s_zb, r_zb, s_g, r_g, s_ids, r_ids,
):
    inst = lax.axis_index("inst")
    lab = lax.axis_index("lab")
    x, c = inst // 2, inst % 2
    z, y = lab // ny, lab % ny
    other = 1 - c
    tile = val_ref.shape[1]
    width = feat_ref.shape[1]
    half = width // 2
    row_tiles = feat_ref.shape[0] // tile
    n_tiles = val_ref.shape[0]
    part = tile // CHUNKS

    core_peer = (x * 2 + other, lab)
    x_at = lambda d: (x + d) % nx
    y_at = lambda d: (y + d) % ny
    zq, zr = z // pair, z % pair
    zq_all = nz // pair
    zb = zq_all * CL_OWN
    lanes = half // PIECES
    zq_at = lambda d: (zq + d) % zq_all
    x_peer = lambda d: (x_at(d) * 2 + c, lab)
    y_peer = lambda d: (inst, z * ny + y_at(d))
    z_peer = lambda d: (inst, (zq_at(d) * pair + zr) * ny + y)
    pair_peer = (inst, (zq * pair + (pair - 1 - zr)) * ny + y)
    peers = [core_peer]
    peers += [x_peer(d) for d in range(1, nx)]
    peers += [y_peer(d) for d in range(1, ny)]
    peers += [z_peer(d) for d in range(1, zq_all)]
    if pair == 2:
        peers.append(pair_peer)

    barrier = pltpu.get_barrier_semaphore()
    for peer in peers:
        pl.semaphore_signal(barrier, inc=1, device_id=peer, device_id_type=MESH)

    def remote(src, dst, send, recv, peer):
        return pltpu.make_async_remote_copy(
            src_ref=src, dst_ref=dst, send_sem=send, recv_sem=recv,
            device_id=peer, device_id_type=MESH,
        )

    sent = []

    xn[...] = unit_rows(feat_ref[...].astype(jnp.float32)).astype(jnp.bfloat16)
    for n in range(n_tiles):
        vt[n] = val_ref[n].T
    vt[n_tiles] = jnp.zeros((tile, tile), jnp.bfloat16)

    def partial(label_tile):
        pieces = []
        for r in range(row_tiles):
            at = jnp.int32(n_tiles)
            for n in range(n_tiles):
                hit = jnp.logical_and(rows_ref[n] == r, labs_ref[n] == label_tile)
                at = jnp.where(hit, n, at)
            pieces.append(vt[at])
        lhs = jnp.concatenate(pieces, axis=1)
        return jnp.dot(lhs, xn[...], preferred_element_type=jnp.float32)

    ids_copy = remote(ids_ref, ids_far, s_ids, r_ids, pair_peer)

    def meet():
        pl.semaphore_wait(barrier, len(peers))
        if pair == 2:
            ids_copy.start()
            sent.append(ids_copy)

    def core_send(d):
        xp = x_at(d)
        csend[xp] = partial(xp * 2 + other).astype(jnp.bfloat16)
        copies = []
        for q in range(CHUNKS):
            rows = pl.ds(q * part, part)
            copy = remote(
                csend.at[xp, rows], crecv.at[xp, rows],
                s_core.at[xp, q], r_core.at[xp, q], core_peer,
            )
            copies.append(copy)
        return copies

    x_copies = {}
    for d in range(1, nx):
        copies = core_send(d)
        if d == 1:
            meet()
        for copy in copies:
            copy.start()
        sent += copies
        total[...] = partial(x_at(d) * 2 + c)
        for q in range(CHUNKS):
            rows = pl.ds(q * part, part)
            copies[q].wait_recv()
            mixed = total[rows] + crecv[x_at(d), rows].astype(jnp.float32)
            xsend[d - 1, rows] = mixed.astype(jnp.bfloat16)
            copy = remote(
                xsend.at[d - 1, rows], xrecv.at[d - 1, rows],
                s_x.at[d - 1, q], r_x.at[d - 1, q], x_peer(d),
            )
            copy.start()
            x_copies[d, q] = copy
            sent.append(copy)
    copies = core_send(0)
    if nx == 1:
        meet()
    for copy in copies:
        copy.start()
    sent += copies
    total[...] = partial(x * 2 + c)
    for q in range(CHUNKS):
        rows = pl.ds(q * part, part)
        copies[q].wait_recv()
        total[rows] += crecv[x, rows].astype(jnp.float32)

    within = (
        lax.broadcasted_iota(jnp.int32, (zq_all, CL_OWN, tile), 0) * (pair * ny * CL_OWN)
        + lax.broadcasted_iota(jnp.int32, (zq_all, CL_OWN, tile), 1)
    )

    def mark(ids, columns):
        for which, cp in enumerate((other, c)):
            for xp in range(nx):
                for yp in range(ny):
                    base = (((xp * 2 + cp) * nz + zr) * ny + yp) * CL_OWN
                    hit = jnp.where(within + base == ids.reshape(1, 1, tile), 1.0, 0.0)
                    picks[which, xp, yp, :, columns] = hit.reshape(zb, tile).astype(jnp.bfloat16)

    gather = []
    mark(ids_ref[...], pl.ds(0, tile))
    if pair == 2:
        ids_copy.wait_recv()
        mark(ids_far[...], pl.ds(tile, tile))

    for q in range(CHUNKS):
        rows = pl.ds(q * part, part)
        value = total[rows]
        for d in range(1, nx):
            x_copies[d, q].wait_recv()
            value += xrecv[d - 1, rows].astype(jnp.float32)
        value = unit_rows(value)
        emb_ref[rows] = value
        ebf[rows] = value.astype(jnp.bfloat16)
        if pair == 2:
            gather.append(
                remote(
                    ebf.at[rows], ebf.at[pl.ds(tile + q * part, part)],
                    s_g.at[q], r_g.at[q], pair_peer,
                )
            )
            gather[-1].start()
    sent += gather

    def sums_a(xp, which):
        member = picks[which, xp].reshape(ny * zb, pair * tile)
        out = jnp.dot(member, ebf[:, :half], preferred_element_type=jnp.float32)
        return out.reshape(ny, zb, half)

    def sums_b(yp, which):
        member = jnp.concatenate([picks[which, xp, yp] for xp in range(nx)], axis=0)
        out = jnp.dot(member, ebf[:, half:], preferred_element_type=jnp.float32)
        return out.reshape(nx, zb, half)

    for copy in gather:
        copy.wait_recv()

    order = [*range(1, max(nx, ny)), 0]
    core_a, core_b = {}, {}
    for d in order:
        if d < nx:
            xp = x_at(d)
            ca_s[xp] = sums_a(xp, 0).astype(jnp.bfloat16)
            core_a[d] = remote(ca_s.at[xp], ca_r.at[xp], s_ca.at[xp], r_ca.at[xp], core_peer)
            core_a[d].start()
        if d < ny:
            yp = y_at(d)
            cb_s[yp] = sums_b(yp, 0).astype(jnp.bfloat16)
            core_b[d] = remote(cb_s.at[yp], cb_r.at[yp], s_cb.at[yp], r_cb.at[yp], core_peer)
            core_b[d].start()
    sent += [*core_a.values(), *core_b.values()]

    xa, yb = {}, {}
    for d in order:
        if d < nx:
            xp = x_at(d)
            mine = sums_a(xp, 1)
            core_a[d].wait_recv()
            mine = mine + ca_r[xp].astype(jnp.float32)
            for p in range(PIECES):
                piece = mine[:, :, p * lanes : (p + 1) * lanes]
                if d:
                    xa_s[d - 1, p] = piece.astype(jnp.bfloat16)
                    xa[d, p] = remote(
                        xa_s.at[d - 1, p], xa_r.at[d - 1, p],
                        s_xa.at[d - 1, p], r_xa.at[d - 1, p], x_peer(d),
                    )
                    xa[d, p].start()
                else:
                    acc_a[p] = piece
        if d < ny:
            yp = y_at(d)
            mine = sums_b(yp, 1)
            core_b[d].wait_recv()
            mine = mine + cb_r[yp].astype(jnp.float32)
            for p in range(PIECES):
                piece = mine[:, :, p * lanes : (p + 1) * lanes]
                if d:
                    yb_s[d - 1, p] = piece.astype(jnp.bfloat16)
                    yb[d, p] = remote(
                        yb_s.at[d - 1, p], yb_r.at[d - 1, p],
                        s_yb.at[d - 1, p], r_yb.at[d - 1, p], y_peer(d),
                    )
                    yb[d, p].start()
                else:
                    acc_b[p] = piece
    sent += [*xa.values(), *yb.values()]

    ya, xb, zs = {}, {}, []

    def second(p):
        for d in range(1, nx):
            xa[d, p].wait_recv()
        for k in range(ny - 1, -1, -1):
            yp = y_at(k)
            mine = acc_a[p, yp]
            for d in range(1, nx):
                mine += xa_r[d - 1, p, yp].astype(jnp.float32)
            if k:
                ya_s[k - 1, p] = mine.astype(jnp.bfloat16)
                ya[k, p] = remote(
                    ya_s.at[k - 1, p], ya_r.at[k - 1, p],
                    s_ya.at[k - 1, p], r_ya.at[k - 1, p], y_peer(k),
                )
                ya[k, p].start()
                sent.append(ya[k, p])
            else:
                fin_a[p] = mine.reshape(zq_all, CL_OWN, lanes)
        for d in range(1, ny):
            yb[d, p].wait_recv()
        for k in range(nx - 1, -1, -1):
            xp = x_at(k)
            mine = acc_b[p, xp]
            for d in range(1, ny):
                mine += yb_r[d - 1, p, xp].astype(jnp.float32)
            if k:
                xb_s[k - 1, p] = mine.astype(jnp.bfloat16)
                xb[k, p] = remote(
                    xb_s.at[k - 1, p], xb_r.at[k - 1, p],
                    s_xb.at[k - 1, p], r_xb.at[k - 1, p], x_peer(k),
                )
                xb[k, p].start()
                sent.append(xb[k, p])
            else:
                fin_b[p] = mine.reshape(zq_all, CL_OWN, lanes)

    def third(p):
        for fin, got, arrived, n_got, z_s, z_r, s_z, r_z in (
            (fin_a, ya, ya_r, ny, za_s, za_r, s_za, r_za),
            (fin_b, xb, xb_r, nx, zb_s, zb_r, s_zb, r_zb),
        ):
            mine = fin[p]
            for k in range(1, n_got):
                got[k, p].wait_recv()
                mine += arrived[k - 1, p].astype(jnp.float32).reshape(zq_all, CL_OWN, lanes)
            fin[p] = mine
            for d in range(1, zq_all):
                z_s[d - 1, p] = fin[p, zq_at(d)].astype(jnp.bfloat16)
                copy = remote(
                    z_s.at[d - 1, p], z_r.at[d - 1, p],
                    s_z.at[d - 1, p], r_z.at[d - 1, p], z_peer(d),
                )
                copy.start()
                zs.append(copy)

    for p in range(PIECES + 1):
        if p < PIECES:
            second(p)
        if p > 0:
            third(p - 1)
    sent += zs

    for copy in zs:
        copy.wait_recv()
    pieces = []
    for fin, z_r in ((fin_a, za_r), (fin_b, zb_r)):
        for p in range(PIECES):
            mine = fin[p, zq]
            for d in range(1, zq_all):
                mine += z_r[d - 1, p].astype(jnp.float32)
            pieces.append(mine)
    cen_ref[...] = unit_rows(jnp.concatenate(pieces, axis=1))

    for copy in sent:
        copy.wait_send()


def shards(features, tile_rows, tile_labels, tile_values, cluster_ids):
    tile = tile_values.shape[1]
    width = features.shape[1]
    labels = cluster_ids.shape[0]
    n_inst, n_lab = lax.axis_size("inst"), lax.axis_size("lab")
    nx = n_inst // 2
    ny = nx if n_lab % nx == 0 else 1
    nz = n_lab // ny
    assert labels == tile
    pair = 2 if nz % 2 == 0 else 1
    zb = nz // pair * CL_OWN
    lanes = width // 2 // PIECES
    half = lanes * PIECES
    bf, f32 = jnp.bfloat16, jnp.float32
    ox, oy, oz = max(nx - 1, 1), max(ny - 1, 1), max(nz // pair - 1, 1)
    dma = lambda *shape: [pltpu.SemaphoreType.DMA(shape)] * 2
    vmem = pl.BlockSpec(memory_space=pltpu.VMEM)
    smem = pl.BlockSpec(memory_space=pltpu.SMEM)
    return pl.pallas_call(
        functools.partial(kernel, nx, ny, nz, pair),
        out_shape=(
            pltpu.VMEM((labels, width), f32),
            pltpu.VMEM((CL_OWN, width), f32),
        ),
        in_specs=[smem, smem, vmem, vmem, vmem],
        out_specs=(vmem, vmem),
        scratch_shapes=[
            pltpu.VMEM(features.shape, bf),
            pltpu.VMEM((tile_values.shape[0] + 1, tile, tile), bf),
            pltpu.VMEM((nx, tile, width), bf),
            pltpu.VMEM((nx, tile, width), bf),
            pltpu.VMEM((ox, tile, width), bf),
            pltpu.VMEM((ox, tile, width), bf),
            pltpu.VMEM((tile, width), f32),
            pltpu.VMEM((pair * tile, width), bf),
            pltpu.VMEM((1, tile), jnp.int32),
            pltpu.VMEM((2, nx, ny, zb, pair * tile), bf),
            pltpu.VMEM((nx, ny, zb, half), bf),
            pltpu.VMEM((nx, ny, zb, half), bf),
            pltpu.VMEM((ox, PIECES, ny, zb, lanes), bf),
            pltpu.VMEM((ox, PIECES, ny, zb, lanes), bf),
            pltpu.VMEM((PIECES, ny, zb, lanes), f32),
            pltpu.VMEM((oy, PIECES, zb, lanes), bf),
            pltpu.VMEM((oy, PIECES, zb, lanes), bf),
            pltpu.VMEM((ny, nx, zb, half), bf),
            pltpu.VMEM((ny, nx, zb, half), bf),
            pltpu.VMEM((oy, PIECES, nx, zb, lanes), bf),
            pltpu.VMEM((oy, PIECES, nx, zb, lanes), bf),
            pltpu.VMEM((PIECES, nx, zb, lanes), f32),
            pltpu.VMEM((ox, PIECES, zb, lanes), bf),
            pltpu.VMEM((ox, PIECES, zb, lanes), bf),
            pltpu.VMEM((PIECES, nz // pair, CL_OWN, lanes), f32),
            pltpu.VMEM((PIECES, nz // pair, CL_OWN, lanes), f32),
            pltpu.VMEM((oz, PIECES, CL_OWN, lanes), bf),
            pltpu.VMEM((oz, PIECES, CL_OWN, lanes), bf),
            pltpu.VMEM((oz, PIECES, CL_OWN, lanes), bf),
            pltpu.VMEM((oz, PIECES, CL_OWN, lanes), bf),
            *dma(nx, CHUNKS),
            *dma(ox, CHUNKS),
            *dma(nx),
            *dma(ny),
            *dma(ox, PIECES),
            *dma(oy, PIECES),
            *dma(oy, PIECES),
            *dma(ox, PIECES),
            *dma(oz, PIECES),
            *dma(oz, PIECES),
            *dma(CHUNKS),
            pltpu.SemaphoreType.DMA,
            pltpu.SemaphoreType.DMA,
        ],
        compiler_params=pltpu.CompilerParams(
            collective_id=0, has_side_effects=True, vmem_limit_bytes=60 * 1024 * 1024
        ),
        name="pifa_step",
    )(tile_rows, tile_labels, cluster_ids.reshape(1, labels), features, tile_values)


def solution(mesh):
    return jax.shard_map(
        shards,
        mesh=mesh,
        in_specs=(
            P("inst", None),
            P(("inst", "lab")),
            P(("inst", "lab")),
            P(("inst", "lab"), None, None),
            P(("lab", "inst")),
        ),
        out_specs=(P(("lab", "inst"), None), P(("inst", "lab"), None)),
        check_vma=False,
    )
```

```python
import functools

import jax
import jax.numpy as jnp
from jax import lax
from jax.experimental import pallas as pl
from jax.experimental.pallas import tpu as pltpu
from jax.sharding import PartitionSpec as P

CL_OWN = 32
CHUNKS = 8
LAG = 3
PIECES = 1
MESH = pl.DeviceIdType.MESH


def unit_rows(matrix):
    return matrix * lax.rsqrt(jnp.sum(matrix * matrix, axis=-1, keepdims=True) + 1e-06)


def kernel(
    nx, ny, nz, pair,
    rows_ref, labs_ref, ids_ref, feat_ref, val_ref,
    emb_ref, cen_ref,
    xn, vt, csend, crecv, xsend, xrecv, total, ebf, ids_far, picks,
    xa_s, xa_r, acc_a, ya_s, ya_r,
    yb_s, yb_r, acc_b, xb_s, xb_r,
    fin_a, fin_b, za_s, za_r, zb_s, zb_r,
    s_core, r_core, s_x, r_x,
    s_xa, r_xa, s_yb, r_yb, s_ya, r_ya, s_xb, r_xb, s_za, r_za, s_zb, r_zb, s_g, r_g, s_ids, r_ids,
):
    inst = lax.axis_index("inst")
    lab = lax.axis_index("lab")
    x, c = inst // 2, inst % 2
    z, y = lab // ny, lab % ny
    other = 1 - c
    tile = val_ref.shape[1]
    width = feat_ref.shape[1]
    half = width // 2
    row_tiles = feat_ref.shape[0] // tile
    n_tiles = val_ref.shape[0]
    part = tile // CHUNKS

    core_peer = (x * 2 + other, lab)
    x_at = lambda d: (x + d) % nx
    y_at = lambda d: (y + d) % ny
    zq, zr = z // pair, z % pair
    zq_all = nz // pair
    zb = zq_all * CL_OWN
    lanes = half // PIECES
    zq_at = lambda d: (zq + d) % zq_all
    x_peer = lambda d: (x_at(d) * 2 + c, lab)
    y_peer = lambda d: (inst, z * ny + y_at(d))
    z_peer = lambda d: (inst, (zq_at(d) * pair + zr) * ny + y)
    pair_peer = (inst, (zq * pair + (pair - 1 - zr)) * ny + y)
    peers = [core_peer]
    peers += [x_peer(d) for d in range(1, nx)]
    peers += [y_peer(d) for d in range(1, ny)]
    peers += [z_peer(d) for d in range(1, zq_all)]
    if pair == 2:
        peers.append(pair_peer)

    barrier = pltpu.get_barrier_semaphore()
    for peer in peers:
        pl.semaphore_signal(barrier, inc=1, device_id=peer, device_id_type=MESH)

    def remote(src, dst, send, recv, peer):
        return pltpu.make_async_remote_copy(
            src_ref=src, dst_ref=dst, send_sem=send, recv_sem=recv,
            device_id=peer, device_id_type=MESH,
        )

    sent = []

    xn[...] = unit_rows(feat_ref[...].astype(jnp.float32)).astype(jnp.bfloat16)
    for n in range(n_tiles):
        vt[n] = val_ref[n].T
    vt[n_tiles] = jnp.zeros((tile, tile), jnp.bfloat16)

    def partial(label_tile):
        pieces = []
        for r in range(row_tiles):
            at = jnp.int32(n_tiles)
            for n in range(n_tiles):
                hit = jnp.logical_and(rows_ref[n] == r, labs_ref[n] == label_tile)
                at = jnp.where(hit, n, at)
            pieces.append(vt[at])
        lhs = jnp.concatenate(pieces, axis=1)
        return jnp.dot(lhs, xn[...], preferred_element_type=jnp.float32)

    def ids_send(source, slot, peer):
        return remote(source, ids_far.at[slot - 1], s_ids.at[slot - 1], r_ids.at[slot - 1], peer)

    ids_sends = {pair: ids_send(ids_ref, pair, core_peer)}
    if pair == 2:
        ids_sends[1] = ids_send(ids_ref, 1, pair_peer)
        ids_sends[3] = ids_send(ids_far.at[0], 3, core_peer)

    def meet():
        pl.semaphore_wait(barrier, len(peers))
        for slot, copy in ids_sends.items():
            if slot <= pair:
                copy.start()

    def core_send(d):
        xp = x_at(d)
        csend[xp] = partial(xp * 2 + other).astype(jnp.bfloat16)
        copies = []
        for q in range(CHUNKS):
            rows = pl.ds(q * part, part)
            copy = remote(
                csend.at[xp, rows], crecv.at[xp, rows],
                s_core.at[xp, q], r_core.at[xp, q], core_peer,
            )
            copies.append(copy)
        return copies

    x_copies = {}
    for d in range(1, nx):
        copies = core_send(d)
        if d == 1:
            meet()
        for copy in copies:
            copy.start()
        sent += copies
        total[...] = partial(x_at(d) * 2 + c)
        for q in range(CHUNKS):
            rows = pl.ds(q * part, part)
            copies[q].wait_recv()
            mixed = total[rows] + crecv[x_at(d), rows].astype(jnp.float32)
            xsend[d - 1, rows] = mixed.astype(jnp.bfloat16)
            copy = remote(
                xsend.at[d - 1, rows], xrecv.at[d - 1, rows],
                s_x.at[d - 1, q], r_x.at[d - 1, q], x_peer(d),
            )
            copy.start()
            x_copies[d, q] = copy
            sent.append(copy)
    copies = core_send(0)
    if nx == 1:
        meet()
    for copy in copies:
        copy.start()
    sent += copies
    total[...] = partial(x * 2 + c)
    for q in range(CHUNKS):
        rows = pl.ds(q * part, part)
        copies[q].wait_recv()
        total[rows] += crecv[x, rows].astype(jnp.float32)

    within = (
        lax.broadcasted_iota(jnp.int32, (zq_all, CL_OWN, tile), 0) * (pair * ny * CL_OWN)
        + lax.broadcasted_iota(jnp.int32, (zq_all, CL_OWN, tile), 1)
    )

    def mark(ids, slot):
        for xp in range(nx):
            for yp in range(ny):
                base = (((xp * 2 + c) * nz + zr) * ny + yp) * CL_OWN
                hit = jnp.where(within + base == ids.reshape(1, 1, tile), 1.0, 0.0)
                picks[xp, yp, :, slot * tile : (slot + 1) * tile] = hit.reshape(
                    zb, tile
                ).astype(jnp.bfloat16)

    mark(ids_ref[...], 0)
    for slot in range(1, 2 * pair):
        ids_sends[slot].wait_recv()
        if slot == 1 and pair == 2:
            ids_sends[3].start()
        mark(ids_far[slot - 1], slot)
    sent += ids_sends.values()

    def row_send(q, source, slot, peer):
        copy = remote(
            ebf.at[pl.ds(source * tile + q * part, part)],
            ebf.at[pl.ds(slot * tile + q * part, part)],
            s_g.at[slot - 1, q], r_g.at[slot - 1, q], peer,
        )
        copy.start()
        gather[slot, q] = copy

    gather = {}

    def relay(q):
        gather[1, q].wait_recv()
        row_send(q, 1, 3, core_peer)

    for q in range(CHUNKS):
        rows = pl.ds(q * part, part)
        value = total[rows]
        for d in range(1, nx):
            x_copies[d, q].wait_recv()
            value += xrecv[d - 1, rows].astype(jnp.float32)
        value = unit_rows(value)
        emb_ref[rows] = value
        ebf[rows] = value.astype(jnp.bfloat16)
        if pair == 2:
            row_send(q, 0, 1, pair_peer)
            if q >= LAG:
                relay(q - LAG)
        row_send(q, 0, pair, core_peer)
    if pair == 2:
        for q in range(max(CHUNKS - LAG, 0), CHUNKS):
            relay(q)
    sent += gather.values()

    def sums_a(xp):
        member = picks[xp].reshape(ny * zb, 2 * pair * tile)
        out = jnp.dot(member, ebf[:, :half], preferred_element_type=jnp.float32)
        return out.reshape(ny, zb, half)

    def sums_b(yp):
        member = jnp.concatenate([picks[xp, yp] for xp in range(nx)], axis=0)
        out = jnp.dot(member, ebf[:, half:], preferred_element_type=jnp.float32)
        return out.reshape(nx, zb, half)

    for (slot, _), copy in gather.items():
        if slot > 1 or pair == 1:
            copy.wait_recv()

    order = [*range(1, max(nx, ny)), 0]
    xa, yb = {}, {}
    for d in order:
        if d < nx:
            xp = x_at(d)
            mine = sums_a(xp)
            for p in range(PIECES):
                piece = mine[:, :, p * lanes : (p + 1) * lanes]
                if d:
                    xa_s[d - 1, p] = piece.astype(jnp.bfloat16)
                    xa[d, p] = remote(
                        xa_s.at[d - 1, p], xa_r.at[d - 1, p],
                        s_xa.at[d - 1, p], r_xa.at[d - 1, p], x_peer(d),
                    )
                    xa[d, p].start()
                else:
                    acc_a[p] = piece
        if d < ny:
            yp = y_at(d)
            mine = sums_b(yp)
            for p in range(PIECES):
                piece = mine[:, :, p * lanes : (p + 1) * lanes]
                if d:
                    yb_s[d - 1, p] = piece.astype(jnp.bfloat16)
                    yb[d, p] = remote(
                        yb_s.at[d - 1, p], yb_r.at[d - 1, p],
                        s_yb.at[d - 1, p], r_yb.at[d - 1, p], y_peer(d),
                    )
                    yb[d, p].start()
                else:
                    acc_b[p] = piece
    sent += [*xa.values(), *yb.values()]

    ya, xb, zs = {}, {}, []

    def second(p):
        for d in range(1, nx):
            xa[d, p].wait_recv()
        for k in range(ny - 1, -1, -1):
            yp = y_at(k)
            mine = acc_a[p, yp]
            for d in range(1, nx):
                mine += xa_r[d - 1, p, yp].astype(jnp.float32)
            if k:
                ya_s[k - 1, p] = mine.astype(jnp.bfloat16)
                ya[k, p] = remote(
                    ya_s.at[k - 1, p], ya_r.at[k - 1, p],
                    s_ya.at[k - 1, p], r_ya.at[k - 1, p], y_peer(k),
                )
                ya[k, p].start()
                sent.append(ya[k, p])
            else:
                fin_a[p] = mine.reshape(zq_all, CL_OWN, lanes)
        for d in range(1, ny):
            yb[d, p].wait_recv()
        for k in range(nx - 1, -1, -1):
            xp = x_at(k)
            mine = acc_b[p, xp]
            for d in range(1, ny):
                mine += yb_r[d - 1, p, xp].astype(jnp.float32)
            if k:
                xb_s[k - 1, p] = mine.astype(jnp.bfloat16)
                xb[k, p] = remote(
                    xb_s.at[k - 1, p], xb_r.at[k - 1, p],
                    s_xb.at[k - 1, p], r_xb.at[k - 1, p], x_peer(k),
                )
                xb[k, p].start()
                sent.append(xb[k, p])
            else:
                fin_b[p] = mine.reshape(zq_all, CL_OWN, lanes)

    def third(p):
        for fin, got, arrived, n_got, z_s, z_r, s_z, r_z in (
            (fin_a, ya, ya_r, ny, za_s, za_r, s_za, r_za),
            (fin_b, xb, xb_r, nx, zb_s, zb_r, s_zb, r_zb),
        ):
            mine = fin[p]
            for k in range(1, n_got):
                got[k, p].wait_recv()
                mine += arrived[k - 1, p].astype(jnp.float32).reshape(zq_all, CL_OWN, lanes)
            fin[p] = mine
            for d in range(1, zq_all):
                z_s[d - 1, p] = fin[p, zq_at(d)].astype(jnp.bfloat16)
                copy = remote(
                    z_s.at[d - 1, p], z_r.at[d - 1, p],
                    s_z.at[d - 1, p], r_z.at[d - 1, p], z_peer(d),
                )
                copy.start()
                zs.append(copy)

    for p in range(PIECES + 1):
        if p < PIECES:
            second(p)
        if p > 0:
            third(p - 1)
    sent += zs

    for copy in zs:
        copy.wait_recv()
    pieces = []
    for fin, z_r in ((fin_a, za_r), (fin_b, zb_r)):
        for p in range(PIECES):
            mine = fin[p, zq]
            for d in range(1, zq_all):
                mine += z_r[d - 1, p].astype(jnp.float32)
            pieces.append(mine)
    cen_ref[...] = unit_rows(jnp.concatenate(pieces, axis=1))

    for copy in sent:
        copy.wait_send()


def shards(features, tile_rows, tile_labels, tile_values, cluster_ids):
    tile = tile_values.shape[1]
    width = features.shape[1]
    labels = cluster_ids.shape[0]
    n_inst, n_lab = lax.axis_size("inst"), lax.axis_size("lab")
    nx = n_inst // 2
    ny = nx if n_lab % nx == 0 else 1
    nz = n_lab // ny
    assert labels == tile
    pair = 2 if nz % 2 == 0 else 1
    zb = nz // pair * CL_OWN
    lanes = width // 2 // PIECES
    half = lanes * PIECES
    bf, f32 = jnp.bfloat16, jnp.float32
    ox, oy, oz = max(nx - 1, 1), max(ny - 1, 1), max(nz // pair - 1, 1)
    dma = lambda *shape: [pltpu.SemaphoreType.DMA(shape)] * 2
    vmem = pl.BlockSpec(memory_space=pltpu.VMEM)
    smem = pl.BlockSpec(memory_space=pltpu.SMEM)
    return pl.pallas_call(
        functools.partial(kernel, nx, ny, nz, pair),
        out_shape=(
            pltpu.VMEM((labels, width), f32),
            pltpu.VMEM((CL_OWN, width), f32),
        ),
        in_specs=[smem, smem, vmem, vmem, vmem],
        out_specs=(vmem, vmem),
        scratch_shapes=[
            pltpu.VMEM(features.shape, bf),
            pltpu.VMEM((tile_values.shape[0] + 1, tile, tile), bf),
            pltpu.VMEM((nx, tile, width), bf),
            pltpu.VMEM((nx, tile, width), bf),
            pltpu.VMEM((ox, tile, width), bf),
            pltpu.VMEM((ox, tile, width), bf),
            pltpu.VMEM((tile, width), f32),
            pltpu.VMEM((2 * pair * tile, width), bf),
            pltpu.VMEM((2 * pair - 1, 1, tile), jnp.int32),
            pltpu.VMEM((nx, ny, zb, 2 * pair * tile), bf),
            pltpu.VMEM((ox, PIECES, ny, zb, lanes), bf),
            pltpu.VMEM((ox, PIECES, ny, zb, lanes), bf),
            pltpu.VMEM((PIECES, ny, zb, lanes), f32),
            pltpu.VMEM((oy, PIECES, zb, lanes), bf),
            pltpu.VMEM((oy, PIECES, zb, lanes), bf),
            pltpu.VMEM((oy, PIECES, nx, zb, lanes), bf),
            pltpu.VMEM((oy, PIECES, nx, zb, lanes), bf),
            pltpu.VMEM((PIECES, nx, zb, lanes), f32),
            pltpu.VMEM((ox, PIECES, zb, lanes), bf),
            pltpu.VMEM((ox, PIECES, zb, lanes), bf),
            pltpu.VMEM((PIECES, nz // pair, CL_OWN, lanes), f32),
            pltpu.VMEM((PIECES, nz // pair, CL_OWN, lanes), f32),
            pltpu.VMEM((oz, PIECES, CL_OWN, lanes), bf),
            pltpu.VMEM((oz, PIECES, CL_OWN, lanes), bf),
            pltpu.VMEM((oz, PIECES, CL_OWN, lanes), bf),
            pltpu.VMEM((oz, PIECES, CL_OWN, lanes), bf),
            *dma(nx, CHUNKS),
            *dma(ox, CHUNKS),
            *dma(ox, PIECES),
            *dma(oy, PIECES),
            *dma(oy, PIECES),
            *dma(ox, PIECES),
            *dma(oz, PIECES),
            *dma(oz, PIECES),
            *dma(2 * pair - 1, CHUNKS),
            *dma(2 * pair - 1),
        ],
        compiler_params=pltpu.CompilerParams(
            collective_id=0, has_side_effects=True, vmem_limit_bytes=60 * 1024 * 1024
        ),
        name="pifa_step",
    )(tile_rows, tile_labels, cluster_ids.reshape(1, labels), features, tile_values)


def solution(mesh):
    return jax.shard_map(
        shards,
        mesh=mesh,
        in_specs=(
            P("inst", None),
            P(("inst", "lab")),
            P(("inst", "lab")),
            P(("inst", "lab"), None, None),
            P(("lab", "inst")),
        ),
        out_specs=(P(("lab", "inst"), None), P(("inst", "lab"), None)),
        check_vma=False,
    )
```

```python
import functools

import jax
import jax.numpy as jnp
from jax import lax
from jax.experimental import pallas as pl
from jax.experimental.pallas import tpu as pltpu
from jax.sharding import PartitionSpec as P

CL_OWN = 32
CHUNKS = 8
LAG = 3
PIECES = 1
MESH = pl.DeviceIdType.MESH


def unit_rows(matrix):
    return matrix * lax.rsqrt(jnp.sum(matrix * matrix, axis=-1, keepdims=True) + 1e-06)


def kernel(
    nx, ny, nz, pair,
    rows_ref, labs_ref, ids_ref, feat_ref, val_ref,
    emb_ref, cen_ref,
    xn, vt, csend, crecv, xsend, xrecv, total, ebf, ids_far, picks, pre_a, pre_b,
    xa_s, xa_r, acc_a, ya_s, ya_r,
    yb_s, yb_r, acc_b, xb_s, xb_r,
    fin_a, fin_b, za_s, za_r, zb_s, zb_r,
    s_core, r_core, s_x, r_x,
    s_xa, r_xa, s_yb, r_yb, s_ya, r_ya, s_xb, r_xb, s_za, r_za, s_zb, r_zb, s_g, r_g, s_ids, r_ids,
):
    inst = lax.axis_index("inst")
    lab = lax.axis_index("lab")
    x, c = inst // 2, inst % 2
    z, y = lab // ny, lab % ny
    other = 1 - c
    tile = val_ref.shape[1]
    width = feat_ref.shape[1]
    half = width // 2
    row_tiles = feat_ref.shape[0] // tile
    n_tiles = val_ref.shape[0]
    part = tile // CHUNKS

    core_peer = (x * 2 + other, lab)
    x_at = lambda d: (x + d) % nx
    y_at = lambda d: (y + d) % ny
    zq, zr = z // pair, z % pair
    zq_all = nz // pair
    zb = zq_all * CL_OWN
    lanes = half // PIECES
    zq_at = lambda d: (zq + d) % zq_all
    x_peer = lambda d: (x_at(d) * 2 + c, lab)
    y_peer = lambda d: (inst, z * ny + y_at(d))
    z_peer = lambda d: (inst, (zq_at(d) * pair + zr) * ny + y)
    pair_peer = (inst, (zq * pair + (pair - 1 - zr)) * ny + y)
    peers = [core_peer]
    peers += [x_peer(d) for d in range(1, nx)]
    peers += [y_peer(d) for d in range(1, ny)]
    peers += [z_peer(d) for d in range(1, zq_all)]
    if pair == 2:
        peers.append(pair_peer)

    barrier = pltpu.get_barrier_semaphore()
    for peer in peers:
        pl.semaphore_signal(barrier, inc=1, device_id=peer, device_id_type=MESH)

    def remote(src, dst, send, recv, peer):
        return pltpu.make_async_remote_copy(
            src_ref=src, dst_ref=dst, send_sem=send, recv_sem=recv,
            device_id=peer, device_id_type=MESH,
        )

    sent = []

    xn[...] = unit_rows(feat_ref[...].astype(jnp.float32)).astype(jnp.bfloat16)
    for n in range(n_tiles):
        vt[n] = val_ref[n].T
    vt[n_tiles] = jnp.zeros((tile, tile), jnp.bfloat16)

    def partial(label_tile):
        pieces = []
        for r in range(row_tiles):
            at = jnp.int32(n_tiles)
            for n in range(n_tiles):
                hit = jnp.logical_and(rows_ref[n] == r, labs_ref[n] == label_tile)
                at = jnp.where(hit, n, at)
            pieces.append(vt[at])
        lhs = jnp.concatenate(pieces, axis=1)
        return jnp.dot(lhs, xn[...], preferred_element_type=jnp.float32)

    def ids_send(source, slot, peer):
        return remote(source, ids_far.at[slot - 1], s_ids.at[slot - 1], r_ids.at[slot - 1], peer)

    ids_sends = {pair: ids_send(ids_ref, pair, core_peer)}
    if pair == 2:
        ids_sends[1] = ids_send(ids_ref, 1, pair_peer)
        ids_sends[3] = ids_send(ids_far.at[0], 3, core_peer)

    def meet():
        pl.semaphore_wait(barrier, len(peers))
        for slot, copy in ids_sends.items():
            if slot <= pair:
                copy.start()

    def core_send(d):
        xp = x_at(d)
        csend[xp] = partial(xp * 2 + other).astype(jnp.bfloat16)
        copies = []
        for q in range(CHUNKS):
            rows = pl.ds(q * part, part)
            copy = remote(
                csend.at[xp, rows], crecv.at[xp, rows],
                s_core.at[xp, q], r_core.at[xp, q], core_peer,
            )
            copies.append(copy)
        return copies

    x_copies = {}
    for d in range(1, nx):
        copies = core_send(d)
        if d == 1:
            meet()
        for copy in copies:
            copy.start()
        sent += copies
        total[...] = partial(x_at(d) * 2 + c)
        for q in range(CHUNKS):
            rows = pl.ds(q * part, part)
            copies[q].wait_recv()
            mixed = total[rows] + crecv[x_at(d), rows].astype(jnp.float32)
            xsend[d - 1, rows] = mixed.astype(jnp.bfloat16)
            copy = remote(
                xsend.at[d - 1, rows], xrecv.at[d - 1, rows],
                s_x.at[d - 1, q], r_x.at[d - 1, q], x_peer(d),
            )
            copy.start()
            x_copies[d, q] = copy
            sent.append(copy)
    copies = core_send(0)
    if nx == 1:
        meet()
    for copy in copies:
        copy.start()
    sent += copies
    total[...] = partial(x * 2 + c)
    for q in range(CHUNKS):
        rows = pl.ds(q * part, part)
        copies[q].wait_recv()
        total[rows] += crecv[x, rows].astype(jnp.float32)

    within = (
        lax.broadcasted_iota(jnp.int32, (zq_all, CL_OWN, tile), 0) * (pair * ny * CL_OWN)
        + lax.broadcasted_iota(jnp.int32, (zq_all, CL_OWN, tile), 1)
    )

    def mark(ids, slot):
        for xp in range(nx):
            for yp in range(ny):
                base = (((xp * 2 + c) * nz + zr) * ny + yp) * CL_OWN
                hit = jnp.where(within + base == ids.reshape(1, 1, tile), 1.0, 0.0)
                picks[xp, yp, :, slot * tile : (slot + 1) * tile] = hit.reshape(
                    zb, tile
                ).astype(jnp.bfloat16)

    mark(ids_ref[...], 0)
    for slot in range(1, 2 * pair):
        ids_sends[slot].wait_recv()
        if slot == 1 and pair == 2:
            ids_sends[3].start()
        mark(ids_far[slot - 1], slot)
    sent += ids_sends.values()

    def row_send(q, source, slot, peer):
        copy = remote(
            ebf.at[pl.ds(source * tile + q * part, part)],
            ebf.at[pl.ds(slot * tile + q * part, part)],
            s_g.at[slot - 1, q], r_g.at[slot - 1, q], peer,
        )
        copy.start()
        gather[slot, q] = copy

    gather = {}

    def sums_a(xp, low, high):
        keys = slice(low * tile, high * tile)
        member = picks[xp, :, :, keys].reshape(ny * zb, (high - low) * tile)
        out = jnp.dot(member, ebf[keys, :half], preferred_element_type=jnp.float32)
        return out.reshape(ny, zb, half)

    def sums_b(yp, low, high):
        keys = slice(low * tile, high * tile)
        member = jnp.concatenate([picks[xp, yp, :, keys] for xp in range(nx)], axis=0)
        out = jnp.dot(member, ebf[keys, half:], preferred_element_type=jnp.float32)
        return out.reshape(nx, zb, half)

    def relay(q):
        gather[1, q].wait_recv()
        row_send(q, 1, 3, core_peer)

    for q in range(CHUNKS):
        rows = pl.ds(q * part, part)
        value = total[rows]
        for d in range(1, nx):
            x_copies[d, q].wait_recv()
            value += xrecv[d - 1, rows].astype(jnp.float32)
        value = unit_rows(value)
        emb_ref[rows] = value
        ebf[rows] = value.astype(jnp.bfloat16)
        if pair == 2:
            row_send(q, 0, 1, pair_peer)
            if q >= LAG:
                relay(q - LAG)
        row_send(q, 0, pair, core_peer)
    for xp in range(nx):
        pre_a[xp] = sums_a(xp, 0, 1)
    for yp in range(ny):
        pre_b[yp] = sums_b(yp, 0, 1)
    if pair == 2:
        for q in range(max(CHUNKS - LAG, 0), CHUNKS):
            relay(q)
        for q in range(CHUNKS):
            gather[2, q].wait_recv()
        for xp in range(nx):
            pre_a[xp] += sums_a(xp, 1, 3)
        for yp in range(ny):
            pre_b[yp] += sums_b(yp, 1, 3)
    sent += gather.values()

    last = 2 * pair - 1
    for (slot, _), copy in gather.items():
        if slot == last:
            copy.wait_recv()

    order = [*range(1, max(nx, ny)), 0]
    xa, yb = {}, {}
    for d in order:
        if d < nx:
            xp = x_at(d)
            mine = pre_a[xp] + sums_a(xp, last, last + 1)
            for p in range(PIECES):
                piece = mine[:, :, p * lanes : (p + 1) * lanes]
                if d:
                    xa_s[d - 1, p] = piece.astype(jnp.bfloat16)
                    xa[d, p] = remote(
                        xa_s.at[d - 1, p], xa_r.at[d - 1, p],
                        s_xa.at[d - 1, p], r_xa.at[d - 1, p], x_peer(d),
                    )
                    xa[d, p].start()
                else:
                    acc_a[p] = piece
        if d < ny:
            yp = y_at(d)
            mine = pre_b[yp] + sums_b(yp, last, last + 1)
            for p in range(PIECES):
                piece = mine[:, :, p * lanes : (p + 1) * lanes]
                if d:
                    yb_s[d - 1, p] = piece.astype(jnp.bfloat16)
                    yb[d, p] = remote(
                        yb_s.at[d - 1, p], yb_r.at[d - 1, p],
                        s_yb.at[d - 1, p], r_yb.at[d - 1, p], y_peer(d),
                    )
                    yb[d, p].start()
                else:
                    acc_b[p] = piece
    sent += [*xa.values(), *yb.values()]

    ya, xb, zs = {}, {}, []

    def second(p):
        for d in range(1, nx):
            xa[d, p].wait_recv()
        for k in range(ny - 1, -1, -1):
            yp = y_at(k)
            mine = acc_a[p, yp]
            for d in range(1, nx):
                mine += xa_r[d - 1, p, yp].astype(jnp.float32)
            if k:
                ya_s[k - 1, p] = mine.astype(jnp.bfloat16)
                ya[k, p] = remote(
                    ya_s.at[k - 1, p], ya_r.at[k - 1, p],
                    s_ya.at[k - 1, p], r_ya.at[k - 1, p], y_peer(k),
                )
                ya[k, p].start()
                sent.append(ya[k, p])
            else:
                fin_a[p] = mine.reshape(zq_all, CL_OWN, lanes)
        for d in range(1, ny):
            yb[d, p].wait_recv()
        for k in range(nx - 1, -1, -1):
            xp = x_at(k)
            mine = acc_b[p, xp]
            for d in range(1, ny):
                mine += yb_r[d - 1, p, xp].astype(jnp.float32)
            if k:
                xb_s[k - 1, p] = mine.astype(jnp.bfloat16)
                xb[k, p] = remote(
                    xb_s.at[k - 1, p], xb_r.at[k - 1, p],
                    s_xb.at[k - 1, p], r_xb.at[k - 1, p], x_peer(k),
                )
                xb[k, p].start()
                sent.append(xb[k, p])
            else:
                fin_b[p] = mine.reshape(zq_all, CL_OWN, lanes)

    def third(p):
        for fin, got, arrived, n_got, z_s, z_r, s_z, r_z in (
            (fin_a, ya, ya_r, ny, za_s, za_r, s_za, r_za),
            (fin_b, xb, xb_r, nx, zb_s, zb_r, s_zb, r_zb),
        ):
            mine = fin[p]
            for k in range(1, n_got):
                got[k, p].wait_recv()
                mine += arrived[k - 1, p].astype(jnp.float32).reshape(zq_all, CL_OWN, lanes)
            fin[p] = mine
            for d in range(1, zq_all):
                z_s[d - 1, p] = fin[p, zq_at(d)].astype(jnp.bfloat16)
                copy = remote(
                    z_s.at[d - 1, p], z_r.at[d - 1, p],
                    s_z.at[d - 1, p], r_z.at[d - 1, p], z_peer(d),
                )
                copy.start()
                zs.append(copy)

    for p in range(PIECES + 1):
        if p < PIECES:
            second(p)
        if p > 0:
            third(p - 1)
    sent += zs

    for copy in zs:
        copy.wait_recv()
    pieces = []
    for fin, z_r in ((fin_a, za_r), (fin_b, zb_r)):
        for p in range(PIECES):
            mine = fin[p, zq]
            for d in range(1, zq_all):
                mine += z_r[d - 1, p].astype(jnp.float32)
            pieces.append(mine)
    cen_ref[...] = unit_rows(jnp.concatenate(pieces, axis=1))

    for copy in sent:
        copy.wait_send()


def shards(features, tile_rows, tile_labels, tile_values, cluster_ids):
    tile = tile_values.shape[1]
    width = features.shape[1]
    labels = cluster_ids.shape[0]
    n_inst, n_lab = lax.axis_size("inst"), lax.axis_size("lab")
    nx = n_inst // 2
    ny = nx if n_lab % nx == 0 else 1
    nz = n_lab // ny
    assert labels == tile
    pair = 2 if nz % 2 == 0 else 1
    zb = nz // pair * CL_OWN
    lanes = width // 2 // PIECES
    half = lanes * PIECES
    bf, f32 = jnp.bfloat16, jnp.float32
    ox, oy, oz = max(nx - 1, 1), max(ny - 1, 1), max(nz // pair - 1, 1)
    dma = lambda *shape: [pltpu.SemaphoreType.DMA(shape)] * 2
    vmem = pl.BlockSpec(memory_space=pltpu.VMEM)
    smem = pl.BlockSpec(memory_space=pltpu.SMEM)
    return pl.pallas_call(
        functools.partial(kernel, nx, ny, nz, pair),
        out_shape=(
            pltpu.VMEM((labels, width), f32),
            pltpu.VMEM((CL_OWN, width), f32),
        ),
        in_specs=[smem, smem, vmem, vmem, vmem],
        out_specs=(vmem, vmem),
        scratch_shapes=[
            pltpu.VMEM(features.shape, bf),
            pltpu.VMEM((tile_values.shape[0] + 1, tile, tile), bf),
            pltpu.VMEM((nx, tile, width), bf),
            pltpu.VMEM((nx, tile, width), bf),
            pltpu.VMEM((ox, tile, width), bf),
            pltpu.VMEM((ox, tile, width), bf),
            pltpu.VMEM((tile, width), f32),
            pltpu.VMEM((2 * pair * tile, width), bf),
            pltpu.VMEM((2 * pair - 1, 1, tile), jnp.int32),
            pltpu.VMEM((nx, ny, zb, 2 * pair * tile), bf),
            pltpu.VMEM((nx, ny, zb, half), f32),
            pltpu.VMEM((ny, nx, zb, half), f32),
            pltpu.VMEM((ox, PIECES, ny, zb, lanes), bf),
            pltpu.VMEM((ox, PIECES, ny, zb, lanes), bf),
            pltpu.VMEM((PIECES, ny, zb, lanes), f32),
            pltpu.VMEM((oy, PIECES, zb, lanes), bf),
            pltpu.VMEM((oy, PIECES, zb, lanes), bf),
            pltpu.VMEM((oy, PIECES, nx, zb, lanes), bf),
            pltpu.VMEM((oy, PIECES, nx, zb, lanes), bf),
            pltpu.VMEM((PIECES, nx, zb, lanes), f32),
            pltpu.VMEM((ox, PIECES, zb, lanes), bf),
            pltpu.VMEM((ox, PIECES, zb, lanes), bf),
            pltpu.VMEM((PIECES, nz // pair, CL_OWN, lanes), f32),
            pltpu.VMEM((PIECES, nz // pair, CL_OWN, lanes), f32),
            pltpu.VMEM((oz, PIECES, CL_OWN, lanes), bf),
            pltpu.VMEM((oz, PIECES, CL_OWN, lanes), bf),
            pltpu.VMEM((oz, PIECES, CL_OWN, lanes), bf),
            pltpu.VMEM((oz, PIECES, CL_OWN, lanes), bf),
            *dma(nx, CHUNKS),
            *dma(ox, CHUNKS),
            *dma(ox, PIECES),
            *dma(oy, PIECES),
            *dma(oy, PIECES),
            *dma(ox, PIECES),
            *dma(oz, PIECES),
            *dma(oz, PIECES),
            *dma(2 * pair - 1, CHUNKS),
            *dma(2 * pair - 1),
        ],
        compiler_params=pltpu.CompilerParams(
            collective_id=0, has_side_effects=True, vmem_limit_bytes=60 * 1024 * 1024
        ),
        name="pifa_step",
    )(tile_rows, tile_labels, cluster_ids.reshape(1, labels), features, tile_values)


def solution(mesh):
    return jax.shard_map(
        shards,
        mesh=mesh,
        in_specs=(
            P("inst", None),
            P(("inst", "lab")),
            P(("inst", "lab")),
            P(("inst", "lab"), None, None),
            P(("lab", "inst")),
        ),
        out_specs=(P(("lab", "inst"), None), P(("inst", "lab"), None)),
        check_vma=False,
    )
```

```python
import functools

import jax
import jax.numpy as jnp
from jax import lax
from jax.experimental import pallas as pl
from jax.experimental.pallas import tpu as pltpu
from jax.sharding import PartitionSpec as P

CL_OWN = 32
CHUNKS = 8
PIECES = 1
MESH = pl.DeviceIdType.MESH


def unit_rows(matrix):
    return matrix * lax.rsqrt(jnp.sum(matrix * matrix, axis=-1, keepdims=True) + 1e-06)


def kernel(
    nx, ny, nz, pair,
    rows_ref, labs_ref, ids_ref, feat_ref, val_ref,
    emb_ref, cen_ref,
    xn, vt, csend, crecv, xsend, xrecv, total, ebf, ids_far, picks,
    ca_s, ca_r, xa_s, xa_r, acc_a, ya_s, ya_r,
    cb_s, cb_r, yb_s, yb_r, acc_b, xb_s, xb_r,
    fin_a, fin_b, za_s, za_r, zb_s, zb_r,
    s_core, r_core, s_x, r_x, s_ca, r_ca, s_cb, r_cb,
    s_xa, r_xa, s_yb, r_yb, s_ya, r_ya, s_xb, r_xb, s_za, r_za, s_zb, r_zb, s_g, r_g, s_ids, r_ids,
):
    inst = lax.axis_index("inst")
    lab = lax.axis_index("lab")
    x, c = inst // 2, inst % 2
    z, y = lab // ny, lab % ny
    other = 1 - c
    tile = val_ref.shape[1]
    width = feat_ref.shape[1]
    half = width // 2
    row_tiles = feat_ref.shape[0] // tile
    n_tiles = val_ref.shape[0]
    part = tile // CHUNKS

    core_peer = (x * 2 + other, lab)
    x_at = lambda d: (x + d) % nx
    y_at = lambda d: (y + d) % ny
    zq, zr = z // pair, z % pair
    zq_all = nz // pair
    zb = zq_all * CL_OWN
    lanes = half // PIECES
    zq_at = lambda d: (zq + d) % zq_all
    x_peer = lambda d: (x_at(d) * 2 + c, lab)
    y_peer = lambda d: (inst, z * ny + y_at(d))
    z_peer = lambda d: (inst, (zq_at(d) * pair + zr) * ny + y)
    pair_peer = (inst, (zq * pair + (pair - 1 - zr)) * ny + y)
    peers = [core_peer]
    peers += [x_peer(d) for d in range(1, nx)]
    peers += [y_peer(d) for d in range(1, ny)]
    peers += [z_peer(d) for d in range(1, zq_all)]
    if pair == 2:
        peers.append(pair_peer)

    barrier = pltpu.get_barrier_semaphore()
    for peer in peers:
        pl.semaphore_signal(barrier, inc=1, device_id=peer, device_id_type=MESH)

    def remote(src, dst, send, recv, peer):
        return pltpu.make_async_remote_copy(
            src_ref=src, dst_ref=dst, send_sem=send, recv_sem=recv,
            device_id=peer, device_id_type=MESH,
        )

    sent = []

    xn[...] = unit_rows(feat_ref[...].astype(jnp.float32)).astype(jnp.bfloat16)
    for n in range(n_tiles):
        vt[n] = val_ref[n].T
    vt[n_tiles] = jnp.zeros((tile, tile), jnp.bfloat16)

    def partial(label_tile):
        pieces = []
        for r in range(row_tiles):
            at = jnp.int32(n_tiles)
            for n in range(n_tiles):
                hit = jnp.logical_and(rows_ref[n] == r, labs_ref[n] == label_tile)
                at = jnp.where(hit, n, at)
            pieces.append(vt[at])
        lhs = jnp.concatenate(pieces, axis=1)
        return jnp.dot(lhs, xn[...], preferred_element_type=jnp.float32)

    ids_copy = remote(ids_ref, ids_far, s_ids, r_ids, pair_peer)

    def meet():
        pl.semaphore_wait(barrier, len(peers))
        if pair == 2:
            ids_copy.start()
            sent.append(ids_copy)

    def core_send(d):
        xp = x_at(d)
        csend[xp] = partial(xp * 2 + other).astype(jnp.bfloat16)
        copies = []
        for q in range(CHUNKS):
            rows = pl.ds(q * part, part)
            copy = remote(
                csend.at[xp, rows], crecv.at[xp, rows],
                s_core.at[xp, q], r_core.at[xp, q], core_peer,
            )
            copies.append(copy)
        return copies

    x_copies = {}
    for d in range(1, nx):
        copies = core_send(d)
        if d == 1:
            meet()
        for copy in copies:
            copy.start()
        sent += copies
        total[...] = partial(x_at(d) * 2 + c)
        for q in range(CHUNKS):
            rows = pl.ds(q * part, part)
            copies[q].wait_recv()
            mixed = total[rows] + crecv[x_at(d), rows].astype(jnp.float32)
            xsend[d - 1, rows] = mixed.astype(jnp.bfloat16)
            copy = remote(
                xsend.at[d - 1, rows], xrecv.at[d - 1, rows],
                s_x.at[d - 1, q], r_x.at[d - 1, q], x_peer(d),
            )
            copy.start()
            x_copies[d, q] = copy
            sent.append(copy)
    copies = core_send(0)
    if nx == 1:
        meet()
    for copy in copies:
        copy.start()
    sent += copies
    total[...] = partial(x * 2 + c)
    for q in range(CHUNKS):
        rows = pl.ds(q * part, part)
        copies[q].wait_recv()
        total[rows] += crecv[x, rows].astype(jnp.float32)

    within = (
        lax.broadcasted_iota(jnp.int32, (zq_all, CL_OWN, tile), 0) * (pair * ny * CL_OWN)
        + lax.broadcasted_iota(jnp.int32, (zq_all, CL_OWN, tile), 1)
    )

    def mark(ids, columns):
        for which, cp in enumerate((other, c)):
            for xp in range(nx):
                for yp in range(ny):
                    base = (((xp * 2 + cp) * nz + zr) * ny + yp) * CL_OWN
                    hit = jnp.where(within + base == ids.reshape(1, 1, tile), 1.0, 0.0)
                    picks[which, xp, yp, :, columns] = hit.reshape(zb, tile).astype(jnp.bfloat16)

    gather = []
    mark(ids_ref[...], pl.ds(0, tile))
    if pair == 2:
        ids_copy.wait_recv()
        mark(ids_far[...], pl.ds(tile, tile))

    for q in range(CHUNKS):
        rows = pl.ds(q * part, part)
        value = total[rows]
        for d in range(1, nx):
            x_copies[d, q].wait_recv()
            value += xrecv[d - 1, rows].astype(jnp.float32)
        value = unit_rows(value)
        emb_ref[rows] = value
        ebf[rows] = value.astype(jnp.bfloat16)
        if pair == 2:
            gather.append(
                remote(
                    ebf.at[rows], ebf.at[pl.ds(tile + q * part, part)],
                    s_g.at[q], r_g.at[q], pair_peer,
                )
            )
            gather[-1].start()
    sent += gather

    def sums_a(xp, which):
        member = picks[which, xp].reshape(ny * zb, pair * tile)
        out = jnp.dot(member, ebf[:, :half], preferred_element_type=jnp.float32)
        return out.reshape(ny, zb, half)

    def sums_b(yp, which):
        member = jnp.concatenate([picks[which, xp, yp] for xp in range(nx)], axis=0)
        out = jnp.dot(member, ebf[:, half:], preferred_element_type=jnp.float32)
        return out.reshape(nx, zb, half)

    for copy in gather:
        copy.wait_recv()

    order = [*range(1, max(nx, ny)), 0]
    core_a, core_b = {}, {}
    for d in order:
        if d < nx:
            xp = x_at(d)
            ca_s[xp] = sums_a(xp, 0).astype(jnp.bfloat16)
            core_a[d] = remote(ca_s.at[xp], ca_r.at[xp], s_ca.at[xp], r_ca.at[xp], core_peer)
            core_a[d].start()
        if d < ny:
            yp = y_at(d)
            cb_s[yp] = sums_b(yp, 0).astype(jnp.bfloat16)
            core_b[d] = remote(cb_s.at[yp], cb_r.at[yp], s_cb.at[yp], r_cb.at[yp], core_peer)
            core_b[d].start()
    sent += [*core_a.values(), *core_b.values()]

    xa, yb = {}, {}
    for d in order:
        if d < nx:
            xp = x_at(d)
            mine = sums_a(xp, 1)
            core_a[d].wait_recv()
            mine = mine + ca_r[xp].astype(jnp.float32)
            for p in range(PIECES):
                piece = mine[:, :, p * lanes : (p + 1) * lanes]
                if d:
                    xa_s[d - 1, p] = piece.astype(jnp.bfloat16)
                    xa[d, p] = remote(
                        xa_s.at[d - 1, p], xa_r.at[d - 1, p],
                        s_xa.at[d - 1, p], r_xa.at[d - 1, p], x_peer(d),
                    )
                    xa[d, p].start()
                else:
                    acc_a[p] = piece
        if d < ny:
            yp = y_at(d)
            mine = sums_b(yp, 1)
            core_b[d].wait_recv()
            mine = mine + cb_r[yp].astype(jnp.float32)
            for p in range(PIECES):
                piece = mine[:, :, p * lanes : (p + 1) * lanes]
                if d:
                    yb_s[d - 1, p] = piece.astype(jnp.bfloat16)
                    yb[d, p] = remote(
                        yb_s.at[d - 1, p], yb_r.at[d - 1, p],
                        s_yb.at[d - 1, p], r_yb.at[d - 1, p], y_peer(d),
                    )
                    yb[d, p].start()
                else:
                    acc_b[p] = piece
    sent += [*xa.values(), *yb.values()]

    ya, xb, zs = {}, {}, []

    def second(p):
        for d in range(1, nx):
            xa[d, p].wait_recv()
        for k in range(ny - 1, -1, -1):
            yp = y_at(k)
            mine = acc_a[p, yp]
            for d in range(1, nx):
                mine += xa_r[d - 1, p, yp].astype(jnp.float32)
            if k:
                ya_s[k - 1, p] = mine.astype(jnp.bfloat16)
                ya[k, p] = remote(
                    ya_s.at[k - 1, p], ya_r.at[k - 1, p],
                    s_ya.at[k - 1, p], r_ya.at[k - 1, p], y_peer(k),
                )
                ya[k, p].start()
                sent.append(ya[k, p])
            else:
                fin_a[p] = mine.reshape(zq_all, CL_OWN, lanes)
        for d in range(1, ny):
            yb[d, p].wait_recv()
        for k in range(nx - 1, -1, -1):
            xp = x_at(k)
            mine = acc_b[p, xp]
            for d in range(1, ny):
                mine += yb_r[d - 1, p, xp].astype(jnp.float32)
            if k:
                xb_s[k - 1, p] = mine.astype(jnp.bfloat16)
                xb[k, p] = remote(
                    xb_s.at[k - 1, p], xb_r.at[k - 1, p],
                    s_xb.at[k - 1, p], r_xb.at[k - 1, p], x_peer(k),
                )
                xb[k, p].start()
                sent.append(xb[k, p])
            else:
                fin_b[p] = mine.reshape(zq_all, CL_OWN, lanes)

    def third(p):
        for fin, got, arrived, n_got, z_s, z_r, s_z, r_z in (
            (fin_a, ya, ya_r, ny, za_s, za_r, s_za, r_za),
            (fin_b, xb, xb_r, nx, zb_s, zb_r, s_zb, r_zb),
        ):
            mine = fin[p]
            for k in range(1, n_got):
                got[k, p].wait_recv()
                mine += arrived[k - 1, p].astype(jnp.float32).reshape(zq_all, CL_OWN, lanes)
            fin[p] = mine
            for d in range(1, zq_all):
                z_s[d - 1, p] = fin[p, zq_at(d)].astype(jnp.bfloat16)
                copy = remote(
                    z_s.at[d - 1, p], z_r.at[d - 1, p],
                    s_z.at[d - 1, p], r_z.at[d - 1, p], z_peer(d),
                )
                copy.start()
                zs.append(copy)

    for p in range(PIECES + 1):
        if p < PIECES:
            second(p)
        if p > 0:
            third(p - 1)
    sent += zs

    for copy in zs:
        copy.wait_recv()
    pieces = []
    for fin, z_r in ((fin_a, za_r), (fin_b, zb_r)):
        for p in range(PIECES):
            mine = fin[p, zq]
            for d in range(1, zq_all):
                mine += z_r[d - 1, p].astype(jnp.float32)
            pieces.append(mine)
    cen_ref[...] = unit_rows(jnp.concatenate(pieces, axis=1))

    for copy in sent:
        copy.wait_send()


def shards(features, tile_rows, tile_labels, tile_values, cluster_ids):
    tile = tile_values.shape[1]
    width = features.shape[1]
    labels = cluster_ids.shape[0]
    n_inst, n_lab = lax.axis_size("inst"), lax.axis_size("lab")
    nx = n_inst // 2
    ny = nx if n_lab % nx == 0 else 1
    nz = n_lab // ny
    assert labels == tile
    pair = 2 if nz % 2 == 0 else 1
    zb = nz // pair * CL_OWN
    lanes = width // 2 // PIECES
    half = lanes * PIECES
    bf, f32 = jnp.bfloat16, jnp.float32
    ox, oy, oz = max(nx - 1, 1), max(ny - 1, 1), max(nz // pair - 1, 1)
    dma = lambda *shape: [pltpu.SemaphoreType.DMA(shape)] * 2
    vmem = pl.BlockSpec(memory_space=pltpu.VMEM)
    smem = pl.BlockSpec(memory_space=pltpu.SMEM)
    return pl.pallas_call(
        functools.partial(kernel, nx, ny, nz, pair),
        out_shape=(
            pltpu.VMEM((labels, width), f32),
            pltpu.VMEM((CL_OWN, width), f32),
        ),
        in_specs=[smem, smem, vmem, vmem, vmem],
        out_specs=(vmem, vmem),
        scratch_shapes=[
            pltpu.VMEM(features.shape, bf),
            pltpu.VMEM((tile_values.shape[0] + 1, tile, tile), bf),
            pltpu.VMEM((nx, tile, width), bf),
            pltpu.VMEM((nx, tile, width), bf),
            pltpu.VMEM((ox, tile, width), bf),
            pltpu.VMEM((ox, tile, width), bf),
            pltpu.VMEM((tile, width), f32),
            pltpu.VMEM((pair * tile, width), bf),
            pltpu.VMEM((1, tile), jnp.int32),
            pltpu.VMEM((2, nx, ny, zb, pair * tile), bf),
            pltpu.VMEM((nx, ny, zb, half), bf),
            pltpu.VMEM((nx, ny, zb, half), bf),
            pltpu.VMEM((ox, PIECES, ny, zb, lanes), bf),
            pltpu.VMEM((ox, PIECES, ny, zb, lanes), bf),
            pltpu.VMEM((PIECES, ny, zb, lanes), f32),
            pltpu.VMEM((oy, PIECES, zb, lanes), bf),
            pltpu.VMEM((oy, PIECES, zb, lanes), bf),
            pltpu.VMEM((ny, nx, zb, half), bf),
            pltpu.VMEM((ny, nx, zb, half), bf),
            pltpu.VMEM((oy, PIECES, nx, zb, lanes), bf),
            pltpu.VMEM((oy, PIECES, nx, zb, lanes), bf),
            pltpu.VMEM((PIECES, nx, zb, lanes), f32),
            pltpu.VMEM((ox, PIECES, zb, lanes), bf),
            pltpu.VMEM((ox, PIECES, zb, lanes), bf),
            pltpu.VMEM((PIECES, nz // pair, CL_OWN, lanes), f32),
            pltpu.VMEM((PIECES, nz // pair, CL_OWN, lanes), f32),
            pltpu.VMEM((oz, PIECES, CL_OWN, lanes), bf),
            pltpu.VMEM((oz, PIECES, CL_OWN, lanes), bf),
            pltpu.VMEM((oz, PIECES, CL_OWN, lanes), bf),
            pltpu.VMEM((oz, PIECES, CL_OWN, lanes), bf),
            *dma(nx, CHUNKS),
            *dma(ox, CHUNKS),
            *dma(nx),
            *dma(ny),
            *dma(ox, PIECES),
            *dma(oy, PIECES),
            *dma(oy, PIECES),
            *dma(ox, PIECES),
            *dma(oz, PIECES),
            *dma(oz, PIECES),
            *dma(CHUNKS),
            pltpu.SemaphoreType.DMA,
            pltpu.SemaphoreType.DMA,
        ],
        compiler_params=pltpu.CompilerParams(
            collective_id=0, has_side_effects=True, vmem_limit_bytes=60 * 1024 * 1024
        ),
        name="pifa_step",
    )(tile_rows, tile_labels, cluster_ids.reshape(1, labels), features, tile_values)


def solution(mesh):
    return jax.shard_map(
        shards,
        mesh=mesh,
        in_specs=(
            P("inst", None),
            P(("inst", "lab")),
            P(("inst", "lab")),
            P(("inst", "lab"), None, None),
            P(("lab", "inst")),
        ),
        out_specs=(P(("lab", "inst"), None), P(("inst", "lab"), None)),
        check_vma=False,
    )
```
